32 devices in a mesh: mem: 8 (over z, y), lat: 4 (over x, core).
Axes of the slice: x: 2, y: 2, z: 4, core: 2. Of those that a mesh axis runs over, the one named last changes fastest.
Arguments:
- replica_variables: float32 [8, 4, 64, 4096], P('mem', None, 'lat'), may hold values from -40 to 40, as said below
- analysis: float32 [4, 64, 4096], P(None, 'lat'), may hold values from -4 to 4
- labels: int32 [64, 32], P('lat'), may hold values from 0 to 7, as said below
- pairing: int32 [8], replicated, may hold values from 0 to 7, as said below
Outputs:
- closing_ensemble_values: float32 [8, 4, 64, 4096], P('mem', None, 'lat')
- factor: float32 [8, 8], P('mem')
The draws below stay inside these ranges and needn't reach their ends.
Inputs may be any that keep to these rules, and one draw needn't show every extreme that they name: `replica_variables`: member fields; the spread of members differs across rows and columns. `labels`: every label value occurs at least once. pairing[pairing[m]] = m and pairing[m] != m for every member m.
All inputs are finite; a program needn't handle non-finite values.
Results may differ from the reference program's by a relative error of at most 0.00015.
Values sent between devices are 32-bit elements; how exact they have to be, the bound alone decides.
A program may use at most 64 MiB of HBM per device.

```python
import jax
import jax.numpy as jnp
from jax import lax

LON = 4096
TILE = 128
REGIONS = 8
STEPS = 3
MEMBERS = 8
NLAT = 64


def draw_replica_variables(key, part):
    keys = jax.random.split(key, 3)
    rows = jnp.arange(NLAT).astype(jnp.float32)
    rising = jnp.exp(jnp.log(3.0) * rows / max(NLAT - 1, 1))
    row_scale = rising * jnp.exp(jax.random.uniform(keys[0], (NLAT,), minval=0.0, maxval=1.15))
    col_scale = jnp.exp(jax.random.uniform(keys[1], (LON,), minval=0.0, maxval=1.15))
    scale = 0.05 * row_scale[:, None] * col_scale[None, :]
    base = jax.random.normal(keys[2], (MEMBERS, 4, NLAT, LON))
    return (base * scale).astype(jnp.float32)


def draw_labels(key, part):
    first_key, second_key = jax.random.split(key, 2)
    tiles = LON // TILE
    base = jax.random.randint(first_key, (NLAT * tiles,), 0, REGIONS).astype(jnp.int32)
    places = jax.random.permutation(second_key, NLAT * tiles)[:REGIONS]
    base = base.at[places].set(jnp.arange(REGIONS, dtype=jnp.int32))
    return base.reshape(NLAT, tiles).astype(jnp.int32)


def draw_pairing(key, part):
    order = jax.random.permutation(key, MEMBERS).astype(jnp.int32)
    evens = order[0::2]
    odds = order[1::2]
    partner = jnp.zeros((MEMBERS,), jnp.int32).at[evens].set(odds).at[odds].set(evens)
    return partner.astype(jnp.int32)


def level_of(rng, shape, cuts, low, high):
    gain = 1.0
    for position, blocks in cuts:
        draws = jax.random.uniform(jax.random.fold_in(jax.random.fold_in(rng, 6), position), (blocks,), jnp.float32, low / len(cuts), high / len(cuts))
        gain = gain * jnp.repeat(jnp.exp(draws), shape[position] // blocks).reshape((-1,) + (1,) * (len(shape) - 1 - position))
    return gain


def gaussian(rng, extent, scale, reach, cuts=(), held_as=jnp.bfloat16):
    loudness = level_of(rng, extent, cuts, -0.22, 0.18) if cuts else 1.0
    values = jax.random.normal(rng, extent, jnp.float32) * scale * loudness
    return jnp.minimum(jnp.maximum(values, -reach), reach).astype(held_as)


def setup_inputs(seed: int = 0) -> dict:
    key_of = jax.random.split(jax.random.key(seed), 5)
    return {
        "replica_variables": draw_replica_variables(jax.random.fold_in(key_of[4], 71), 0),
        "analysis": gaussian(key_of[1], (4, NLAT, LON), 0.5, 4.0, ((1, 4),), jnp.float32),
        "labels": draw_labels(jax.random.fold_in(key_of[4], 71), 0),
        "pairing": draw_pairing(jax.random.fold_in(key_of[4], 71), 0),
    }


grav_coef = 0.1
depth_coef = 0.1
advect_coef = 0.05
diffuse_coef = 0.05
coriolis_coef = 0.05
target_size = 0.5
small_eps = 1e-06

def diff_lon(field):
    return jnp.roll(field, -1, axis=-1) - jnp.roll(field, 1, axis=-1)

def trimmed_latitude_lines(field, have, want, offset=0):
    margin = have - want
    total = field.shape[-2]
    return field[..., margin + offset:total - margin + offset, :]

def model_step(extended, have, coriolis, height_rim):
    height = extended[:, 0]
    zonal = extended[:, 1]
    meridional = extended[:, 2]
    tracer = extended[:, 3]
    inner = have - 1
    new_height = trimmed_latitude_lines(height, have, inner) - depth_coef * (diff_lon(trimmed_latitude_lines(zonal, have, inner)) + trimmed_latitude_lines(meridional, have, inner, 1) - trimmed_latitude_lines(meridional, have, inner, -1))
    new_zonal = trimmed_latitude_lines(zonal, have, inner) + trimmed_latitude_lines(coriolis, have, inner) * trimmed_latitude_lines(meridional, have, inner) - grav_coef * diff_lon(new_height)
    padded_height, height_have = height_rim(new_height, inner)
    outer = height_have - 1
    zonal_out = trimmed_latitude_lines(new_zonal, inner, outer)
    new_meridional = trimmed_latitude_lines(meridional, have, outer) - trimmed_latitude_lines(coriolis, have, outer) * zonal_out - grav_coef * (trimmed_latitude_lines(padded_height, height_have, outer, 1) - trimmed_latitude_lines(padded_height, height_have, outer, -1))
    centre = trimmed_latitude_lines(tracer, have, outer)
    upper = trimmed_latitude_lines(tracer, have, outer, 1)
    lower = trimmed_latitude_lines(tracer, have, outer, -1)
    new_tracer = centre - advect_coef * (zonal_out * diff_lon(centre) + new_meridional * (upper - lower)) + diffuse_coef * (jnp.roll(centre, -1, axis=-1) + jnp.roll(centre, 1, axis=-1) + upper + lower - 4.0 * centre)
    quantity_bundle = jnp.stack([trimmed_latitude_lines(padded_height, height_have, outer), zonal_out, new_meridional, new_tracer], axis=1)
    return (quantity_bundle, outer)

def height_with_halo(new_height, have):
    return (jnp.pad(new_height, ((0, 0), (1, 1), (0, 0))), have + 1)

def predicted_flow(quantity_bundle):
    rows_all = quantity_bundle.shape[2]
    global_rows = jnp.arange(-1, rows_all + 1).astype(jnp.float32)
    coriolis = (coriolis_coef * (2.0 * (global_rows + 0.5) / rows_all - 1.0))[:, None]
    for index in range(STEPS):
        extended = jnp.pad(quantity_bundle, ((0, 0), (0, 0), (1, 1), (0, 0)))
        quantity_bundle, _ = model_step(extended, 1, coriolis, height_with_halo)
    return quantity_bundle

def reference(replica_variables, analysis, labels, pairing):
    leading_replica = predicted_flow(replica_variables)
    partner = leading_replica[pairing]
    spread = 0.5 * (leading_replica - partner)
    energy = 0.5 * lax.optimization_barrier(jnp.sum(spread * spread, axis=1))
    padded = jnp.pad(energy, ((0, 0), (1, 1), (0, 0)))
    smoothed_field = 0.25 * (padded[:, 2:] + 2.0 * energy + padded[:, :-2])
    members, rows_all, width = smoothed_field.shape
    tiles = width // TILE
    tile_sums = smoothed_field.reshape(members, rows_all, tiles, TILE).sum(-1)
    onehot = (labels[..., None] == jnp.arange(REGIONS, dtype=jnp.int32)).astype(jnp.float32)
    region_sum = jnp.einsum('mrt,rtk->mk', tile_sums, onehot, precision=lax.Precision.HIGHEST)
    cells = onehot.sum((0, 1)) * TILE
    factor = target_size / jnp.sqrt(region_sum / cells + small_eps)
    cell_factor = jnp.einsum('mk,rtk->mrt', factor, onehot, precision=lax.Precision.HIGHEST)
    scaled = (spread.reshape(members, 4, rows_all, tiles, TILE) * cell_factor[:, None, :, :, None]).reshape(spread.shape)
    central_latitude_lines = analysis[None] + scaled
    closing_ensemble_values = predicted_flow(central_latitude_lines)
    return (closing_ensemble_values, factor)
```

```python
import functools

import jax
import numpy as np
import jax.numpy as jnp
from jax import lax
from jax.sharding import PartitionSpec as P

TILE = 128
REGIONS = 8
STEPS = 3


grav_coef = 0.1
depth_coef = 0.1
advect_coef = 0.05
diffuse_coef = 0.05
coriolis_coef = 0.05
target_size = 0.5
small_eps = 1e-06


def with_halo(array, sides, width):
    for axis, dim in sides:
        size, length = (lax.axis_size(axis), array.shape[dim])
        up = [(i, (i + 1) % size) for i in range(size - 1)]
        down = [(j, i) for i, j in up]
        last = lax.slice_in_dim(array, length - width, length, axis=dim)
        initial = lax.slice_in_dim(array, 0, width, axis=dim)
        before = lax.ppermute(last, axis, up)
        after = lax.ppermute(initial, axis, down)
        array = jnp.concatenate([before, array, after], axis=dim)
    return array


def diff_lon(field):
    return jnp.roll(field, -1, axis=-1) - jnp.roll(field, 1, axis=-1)


def trimmed_latitude_lines(field, have, want, offset=0):
    margin = have - want
    total = field.shape[-2]
    return field[..., margin + offset : total - margin + offset, :]


def model_step(extended, have, coriolis, height_rim):
    height = extended[:, 0]
    zonal = extended[:, 1]
    meridional = extended[:, 2]
    tracer = extended[:, 3]
    inner = have - 1
    new_height = trimmed_latitude_lines(height, have, inner) - depth_coef * (
        diff_lon(trimmed_latitude_lines(zonal, have, inner))
        + trimmed_latitude_lines(meridional, have, inner, 1)
        - trimmed_latitude_lines(meridional, have, inner, -1)
    )
    new_zonal = (
        trimmed_latitude_lines(zonal, have, inner)
        + trimmed_latitude_lines(coriolis, have, inner)
        * trimmed_latitude_lines(meridional, have, inner)
        - grav_coef * diff_lon(new_height)
    )
    padded_height, height_have = height_rim(new_height, inner)
    outer = height_have - 1
    zonal_out = trimmed_latitude_lines(new_zonal, inner, outer)
    new_meridional = (
        trimmed_latitude_lines(meridional, have, outer)
        - trimmed_latitude_lines(coriolis, have, outer) * zonal_out
        - grav_coef
        * (
            trimmed_latitude_lines(padded_height, height_have, outer, 1)
            - trimmed_latitude_lines(padded_height, height_have, outer, -1)
        )
    )
    centre = trimmed_latitude_lines(tracer, have, outer)
    upper = trimmed_latitude_lines(tracer, have, outer, 1)
    lower = trimmed_latitude_lines(tracer, have, outer, -1)
    new_tracer = (
        centre
        - advect_coef * (zonal_out * diff_lon(centre) + new_meridional * (upper - lower))
        + diffuse_coef
        * (
            jnp.roll(centre, -1, axis=-1)
            + jnp.roll(centre, 1, axis=-1)
            + upper
            + lower
            - 4.0 * centre
        )
    )
    quantity_bundle = jnp.stack(
        [
            trimmed_latitude_lines(padded_height, height_have, outer),
            zonal_out,
            new_meridional,
            new_tracer,
        ],
        axis=1,
    )
    return (quantity_bundle, outer)


def global_rows(local_rows, extra):
    start = lax.axis_index("lat") * local_rows
    return (start - extra + jnp.arange(local_rows + 2 * extra)).astype(jnp.float32)


def coriolis_rows(local_rows, extra):
    rows_all = local_rows * lax.axis_size("lat")
    where_rows = global_rows(local_rows, extra)
    return (coriolis_coef * (2.0 * (where_rows + 0.5) / rows_all - 1.0))[:, None]


def inside_latitude_lines(local_rows, extra):
    rows_all = local_rows * lax.axis_size("lat")
    where_rows = global_rows(local_rows, extra)
    return ((where_rows >= 0.0) & (where_rows < rows_all)).astype(jnp.float32)[:, None]


def predicted_flow(quantity_bundle):
    local_rows = quantity_bundle.shape[2]
    depth = 2 * STEPS
    extended = with_halo(quantity_bundle, (("lat", 2),), depth)
    coriolis = coriolis_rows(local_rows, depth)
    have = depth

    def masked_height(new_height, inner):
        keep = trimmed_latitude_lines(inside_latitude_lines(local_rows, depth), depth, inner)
        return (new_height * keep, inner)

    for index in range(STEPS):
        local_coriolis = trimmed_latitude_lines(coriolis, depth, have)
        extended, have = model_step(extended, have, local_coriolis, masked_height)
        extended = extended * trimmed_latitude_lines(
            inside_latitude_lines(local_rows, depth), depth, have
        )
    return extended


def region_weights(tile_labels):
    regions = jnp.arange(REGIONS, dtype=jnp.int32)
    size = lax.axis_size("lat")
    up = [(i, (i + 1) % size) for i in range(size - 1)]
    down = [(j, i) for i, j in up]
    shifted = tile_labels + 1
    before = lax.ppermute(shifted[-1:], "lat", up)
    after = lax.ppermute(shifted[:1], "lat", down)
    padded = jnp.concatenate([before, shifted, after], axis=0) - 1
    onehot = (padded[..., None] == regions).astype(jnp.float32)
    return onehot[1:-1], 0.25 * (onehot[:-2] + 2.0 * onehot[1:-1] + onehot[2:])


def energy_tiles(spread, onehot, weights):
    energy = 0.5 * jnp.sum(spread * spread, axis=1)
    members, local_rows, width = energy.shape
    tile_sums = energy.reshape(members, local_rows, width // TILE, TILE).sum(-1)
    region_sum = jnp.einsum("mrt,rtk->mk", tile_sums, weights, precision=lax.Precision.HIGHEST)
    cells = onehot.sum((0, 1)) * TILE
    return (region_sum, cells)


def matchings(items):
    if not items:
        return [[]]
    first, rest = items[0], items[1:]
    return [
        [(first, other)] + tail
        for i, other in enumerate(rest)
        for tail in matchings(rest[:i] + rest[i + 1 :])
    ]


def matchings_count(size):
    count = 1
    for i in range(size - 1, 0, -2):
        count *= i
    return count


def partner_fields(fields, pairing):
    size = lax.axis_size("mem")
    if matchings_count(size) > 512:
        piece = lax.all_gather(fields, "mem", axis=0, tiled=True)
        partner_index = pairing[lax.axis_index("mem")]
        return lax.dynamic_index_in_dim(piece, partner_index, 0, keepdims=True)
    perms = [
        [(i, j) for i, j in match] + [(j, i) for i, j in match]
        for match in matchings(list(range(size)))
    ]
    table = np.zeros((len(perms), size), np.int32)
    for row, perm in enumerate(perms):
        for i, j in perm:
            table[row, i] = j
    hits = jnp.all(jnp.asarray(table) == pairing[None], axis=1)
    index = jnp.sum(jnp.where(hits, jnp.arange(len(perms), dtype=jnp.int32), 0))
    branches = [functools.partial(lax.ppermute, axis_name="mem", perm=perm) for perm in perms]
    return lax.switch(index, branches, fields)


def recentre(spread, centre_fields, region_sum, cells, onehot):
    factor = target_size / jnp.sqrt(region_sum / cells + small_eps)
    cell_factor = jnp.einsum("mk,rtk->mrt", factor, onehot, precision=lax.Precision.HIGHEST)
    members, fields_count, local_rows, width = spread.shape
    scaled = (
        spread.reshape(members, fields_count, local_rows, width // TILE, TILE)
        * cell_factor[:, None, :, :, None]
    ).reshape(spread.shape)
    return (centre_fields[None] + scaled, factor)


def local(replica_variables, analysis, labels, pairing):
    onehot, weights = region_weights(labels)
    leading_replica = predicted_flow(replica_variables)
    spread = 0.5 * (leading_replica - partner_fields(leading_replica, pairing))
    region_sum, cells = energy_tiles(spread, onehot, weights)
    region_sum, cells = lax.psum((region_sum, cells), "lat")
    central_latitude_lines, factor = recentre(spread, analysis, region_sum, cells, onehot)
    closing_ensemble_values = predicted_flow(central_latitude_lines)
    return (closing_ensemble_values, factor)


def solution(mesh):
    return jax.shard_map(
        local,
        mesh=mesh,
        in_specs=(P("mem", None, "lat", None), P(None, "lat", None), P("lat", None), P()),
        out_specs=(P("mem", None, "lat", None), P("mem", None)),
        check_vma=False,
    )
```

```python
import functools

import jax
import numpy as np
import jax.numpy as jnp
from jax import lax
from jax.experimental import pallas as pl
from jax.experimental.pallas import tpu as pltpu
from jax.sharding import PartitionSpec as P

MESH = pl.DeviceIdType.MESH
TILE = 128
REGIONS = 8
STEPS = 3
HALO = 2 * STEPS
FIELDS = 4
UNROLL = 2
REACH = (2 * STEPS - 1, 2 * STEPS - 1, 2 * STEPS, STEPS)


grav_coef = 0.1
depth_coef = 0.1
advect_coef = 0.05
diffuse_coef = 0.05
coriolis_coef = 0.05
target_size = 0.5
small_eps = 1e-06


def shift_lon(plane):
    sub = plane.shape[0]
    lane = lax.broadcasted_iota(jnp.int32, plane.shape, 1)
    east = pltpu.roll(plane, TILE - 1, 1)
    east = jnp.where(lane == TILE - 1, pltpu.roll(east, sub - 1, 0), east)
    west = pltpu.roll(plane, 1, 1)
    west = jnp.where(lane == 0, pltpu.roll(west, 1, 0), west)
    return east, west


def diff_lon(plane):
    east, west = shift_lon(plane)
    return east - west


def over_rows(first, last, body, count=UNROLL):
    def trip(i, carry):
        body([first + i * count + j for j in range(count)])
        return carry

    lax.fori_loop(0, (last - first) // count, trip, 0)


def run_steps(buf, spare, local_rows, sub, start, rows_all):
    extent = local_rows + 2 * HALO

    def at(field, e):
        return pl.ds(pl.multiple_of((field * extent + e) * sub, sub), sub)

    def inside(e):
        row = start + e - HALO
        return jnp.where((row >= 0) & (row < rows_all), 1.0, 0.0).astype(jnp.float32)

    def coriolis(e):
        row = (start + e - HALO).astype(jnp.float32)
        return coriolis_coef * (2.0 * (row + 0.5) / rows_all - 1.0)

    for step in range(STEPS):
        margin = 2 * (STEPS - 1 - step)
        narrow = STEPS - 1 - step
        source, target = (buf, spare) if step % 2 == 0 else (spare, buf)
        source_field, target_field = (3, 0) if step % 2 == 0 else (0, 3)

        def height(es):
            out = []
            for e in es:
                divergence = diff_lon(buf[at(1, e), :]) + buf[at(2, e + 1), :] - buf[at(2, e - 1), :]
                out.append(inside(e) * (buf[at(0, e), :] - depth_coef * divergence))
            for e, value in zip(es, out):
                buf[at(0, e), :] = value

        def wind(es):
            out = []
            for e in es:
                f = coriolis(e)
                v = buf[at(2, e), :]
                u1 = buf[at(1, e), :] + f * v - grav_coef * diff_lon(buf[at(0, e), :])
                slope = buf[at(0, e + 1), :] - buf[at(0, e - 1), :]
                out.append((u1, inside(e) * (v - f * u1 - grav_coef * slope)))
            for e, (u1, v1) in zip(es, out):
                buf[at(1, e), :] = u1
                buf[at(2, e), :] = v1

        def tracer(es):
            out = []
            for e in es:
                q = source[at(source_field, e), :]
                upper = source[at(source_field, e + 1), :]
                lower = source[at(source_field, e - 1), :]
                east, west = shift_lon(q)
                advected = buf[at(1, e), :] * (east - west) + buf[at(2, e), :] * (upper - lower)
                spreading = east + west + upper + lower - 4.0 * q
                out.append(inside(e) * (q - advect_coef * advected + diffuse_coef * spreading))
            for e, value in zip(es, out):
                target[at(target_field, e), :] = value

        own = (HALO, HALO + local_rows)
        over_rows(own[0] - margin - 1, own[1] + margin + 1, height)
        over_rows(own[0] - margin, own[1] + margin, wind)
        over_rows(own[0] - narrow, own[1] + narrow, tracer)
    return (spare, 0) if STEPS % 2 else (buf, 3)


def halo_copies(buf, local_rows, sub, lat, size, send_sem, recv_sem):
    extent = local_rows + 2 * HALO
    mem = lax.axis_index("mem")
    copies = []
    for side, peer in ((0, lat - 1), (1, lat + 1)):
        group = []
        for field in range(FIELDS):
            reach = REACH[field]
            source = HALO if side == 0 else HALO + local_rows - reach
            target = HALO + local_rows if side == 0 else HALO - reach
            group.append(
                pltpu.make_async_remote_copy(
                    src_ref=buf.at[pl.ds((field * extent + source) * sub, reach * sub), :],
                    dst_ref=buf.at[pl.ds((field * extent + target) * sub, reach * sub), :],
                    send_sem=send_sem.at[side, field],
                    recv_sem=recv_sem.at[side, field],
                    device_id=(mem, peer),
                    device_id_type=MESH,
                )
            )
        copies.append(group)
    return copies


def clear_outside(buf, local_rows, sub, lat, size):
    extent = local_rows + 2 * HALO
    zeros = jnp.zeros((HALO * sub, TILE), jnp.float32)

    @pl.when(lat == 0)
    def _():
        for field in range(FIELDS):
            buf[pl.ds(field * extent * sub, HALO * sub), :] = zeros

    @pl.when(lat == size - 1)
    def _():
        for field in range(FIELDS):
            buf[pl.ds((field * extent + HALO + local_rows) * sub, HALO * sub), :] = zeros


def start_halo(copies, lat, size):
    for side, has in ((0, lat > 0), (1, lat < size - 1)):

        @pl.when(has)
        def _(side=side):
            for copy in copies[side]:
                copy.start()


def finish_halo(copies, lat, size):
    for side, has in ((0, lat > 0), (1, lat < size - 1)):

        @pl.when(has)
        def _(side=side):
            for copy in copies[side]:
                copy.wait_send()
            for copy in copies[1 - side]:
                copy.wait_recv()


def planes_from_rows(source, buf, local_rows, sub):
    extent = local_rows + 2 * HALO
    for field in range(FIELDS):
        for row in range(0, local_rows, 8):
            for t in range(sub):
                first = (field * extent + HALO + row) * sub + t
                buf[pl.ds(first, 8, stride=sub), :] = source[field, row : row + 8, t * TILE : (t + 1) * TILE]


def first_kernel(size, local_rows, sub, x_ref, lab_ref, out_ref, edge_ref, buf, spare, send_sem, recv_sem, lab_send, lab_recv):
    lat = lax.axis_index("lat")
    mem = lax.axis_index("mem")
    extent = local_rows + 2 * HALO
    barrier = pltpu.get_barrier_semaphore()
    for peer, has in ((lat - 1, lat > 0), (lat + 1, lat < size - 1)):

        @pl.when(has)
        def _(peer=peer):
            pl.semaphore_signal(barrier, inc=1, device_id=(mem, peer), device_id_type=MESH)

    clear_outside(buf, local_rows, sub, lat, size)
    planes_from_rows(x_ref, buf, local_rows, sub)
    none = jnp.full((sub, TILE), -1.0, jnp.float32)

    @pl.when(lat == 0)
    def _():
        edge_ref[0] = none

    @pl.when(lat == size - 1)
    def _():
        edge_ref[1] = none

    inner = (lat > 0) & (lat < size - 1)

    @pl.when(inner)
    def _():
        pl.semaphore_wait(barrier, 2)

    @pl.when(jnp.logical_not(inner))
    def _():
        pl.semaphore_wait(barrier, 1)

    copies = halo_copies(buf, local_rows, sub, lat, size, send_sem, recv_sem)
    for side, peer in ((0, lat - 1), (1, lat + 1)):
        row = 0 if side == 0 else local_rows - 1
        copies[side].append(
            pltpu.make_async_remote_copy(
                src_ref=lab_ref.at[row],
                dst_ref=edge_ref.at[1 - side],
                send_sem=lab_send.at[side],
                recv_sem=lab_recv.at[side],
                device_id=(mem, peer),
                device_id_type=MESH,
            )
        )
    start_halo(copies, lat, size)
    finish_halo(copies, lat, size)
    tracer, tracer_field = run_steps(buf, spare, local_rows, sub, lat * local_rows, local_rows * size)
    for field in range(FIELDS):
        ref, place = (tracer, tracer_field) if field == 3 else (buf, field)
        out_ref[field] = ref[pl.ds((place * extent + HALO) * sub, local_rows * sub), :].reshape(local_rows, sub, TILE)


def second_kernel(
    size, local_rows, sub, first_ref, partner_ref, analysis_ref, lab_ref, edge_ref, out_ref, factor_ref,
    buf, spare, spread, sums, send_sem, recv_sem, sum_send, sum_recv,
):
    lat = lax.axis_index("lat")
    mem = lax.axis_index("mem")
    extent = local_rows + 2 * HALO
    barrier = pltpu.get_barrier_semaphore()
    for hop in range(1, size):
        pl.semaphore_signal(barrier, inc=1, device_id=(mem, lax.rem(lat + hop, size)), device_id_type=MESH)

    def fold(plane):
        total = plane[0:8]
        for i in range(8, sub, 8):
            total = total + plane[i : i + 8]
        return total

    energies = [jnp.zeros((8, TILE), jnp.float32) for _ in range(REGIONS)]
    counts = [jnp.zeros((8, TILE), jnp.float32) for _ in range(REGIONS)]

    def accumulate(row, carry):
        energies, counts = carry
        total = jnp.zeros((sub, TILE), jnp.float32)
        for field in range(FIELDS):
            half = 0.5 * (first_ref[field, row] - partner_ref[field, row])
            spread[field, row] = half
            total = total + half * half
        quarter = 0.125 * total
        here = lab_ref[row]
        before = jnp.where(row == 0, edge_ref[0], lab_ref[jnp.maximum(row - 1, 0)])
        after = jnp.where(row == local_rows - 1, edge_ref[1], lab_ref[jnp.minimum(row + 1, local_rows - 1)])
        new_energies, new_counts = [], []
        for k in range(REGIONS):
            kept = jnp.where(here == k, 1.0, 0.0)
            weight = 2.0 * kept + jnp.where(before == k, 1.0, 0.0) + jnp.where(after == k, 1.0, 0.0)
            new_energies.append(energies[k] + fold(quarter * weight))
            new_counts.append(counts[k] + fold(kept))
        return new_energies, new_counts

    energies, counts = lax.fori_loop(0, local_rows, accumulate, (energies, counts))
    for k in range(REGIONS):
        sums[0, k : k + 1, :] = jnp.sum(energies[k], axis=0, keepdims=True)
        sums[0, REGIONS + k : REGIONS + k + 1, :] = jnp.sum(counts[k], axis=0, keepdims=True)

    pl.semaphore_wait(barrier, size - 1)
    sends = []
    for hop in range(1, size):
        sends.append(
            pltpu.make_async_remote_copy(
                src_ref=sums.at[0],
                dst_ref=sums.at[hop],
                send_sem=sum_send.at[hop],
                recv_sem=sum_recv.at[hop],
                device_id=(mem, lax.rem(lat + hop, size)),
                device_id_type=MESH,
            )
        )
    for copy in sends:
        copy.start()
    clear_outside(buf, local_rows, sub, lat, size)
    planes_from_rows(analysis_ref, buf, local_rows, sub)
    for copy in sends:
        copy.wait()
    total = sums[0]
    for hop in range(1, size):
        total = total + sums[hop]
    total = jnp.sum(total, axis=1, keepdims=True)
    factor = target_size / jnp.sqrt(total[:REGIONS] / total[REGIONS:] + small_eps)
    wide = jnp.broadcast_to(factor, (REGIONS, TILE))
    diagonal = lax.broadcasted_iota(jnp.int32, (REGIONS, TILE), 0) == lax.broadcasted_iota(
        jnp.int32, (REGIONS, TILE), 1
    )
    factor_ref[...] = jnp.sum(jnp.where(diagonal, wide, 0.0), axis=0, keepdims=True)[:, :REGIONS]
    lanes = [jnp.broadcast_to(wide[k : k + 1], (sub, TILE)) for k in range(REGIONS)]

    def middle(row, carry):
        here = lab_ref[row]
        scale = lanes[0]
        for k in range(1, REGIONS):
            scale = jnp.where(here == k, lanes[k], scale)
        for field in range(FIELDS):
            place = pl.ds(pl.multiple_of((field * extent + HALO + row) * sub, sub), sub)
            buf[place, :] = buf[place, :] + scale * spread[field, row]
        return carry

    lax.fori_loop(0, local_rows, middle, 0)
    copies = halo_copies(buf, local_rows, sub, lat, size, send_sem, recv_sem)
    start_halo(copies, lat, size)
    finish_halo(copies, lat, size)
    tracer, tracer_field = run_steps(buf, spare, local_rows, sub, lat * local_rows, local_rows * size)
    for field in range(FIELDS):
        ref, place = (tracer, tracer_field) if field == 3 else (buf, field)
        for row in range(0, local_rows, 8):
            for t in range(sub):
                first = (place * extent + HALO + row) * sub + t
                out_ref[field, row : row + 8, t * TILE : (t + 1) * TILE] = ref[pl.ds(first, 8, stride=sub), :]


def matchings(items):
    if not items:
        return [[]]
    first, rest = items[0], items[1:]
    return [
        [(first, other)] + tail
        for i, other in enumerate(rest)
        for tail in matchings(rest[:i] + rest[i + 1 :])
    ]


def matchings_count(size):
    count = 1
    for i in range(size - 1, 0, -2):
        count *= i
    return count


def partner_fields(fields, pairing):
    size = lax.axis_size("mem")
    if matchings_count(size) > 512:
        piece = lax.all_gather(fields, "mem", axis=0, tiled=True)
        partner_index = pairing[lax.axis_index("mem")]
        return lax.dynamic_index_in_dim(piece, partner_index, 0, keepdims=True)
    perms = [
        [(i, j) for i, j in match] + [(j, i) for i, j in match]
        for match in matchings(list(range(size)))
    ]
    table = np.zeros((len(perms), size), np.int32)
    for row, perm in enumerate(perms):
        for i, j in perm:
            table[row, i] = j
    hits = jnp.all(jnp.asarray(table) == pairing[None], axis=1)
    index = jnp.sum(jnp.where(hits, jnp.arange(len(perms), dtype=jnp.int32), 0))
    branches = [functools.partial(lax.ppermute, axis_name="mem", perm=perm) for perm in perms]
    return lax.switch(index, branches, fields)


def recentre(spread, centre_fields, region_sum, cells, onehot):
    factor = target_size / jnp.sqrt(region_sum / cells + small_eps)
    cell_factor = jnp.einsum("mk,rtk->mrt", factor, onehot, precision=lax.Precision.HIGHEST)
    members, fields_count, local_rows, width = spread.shape
    scaled = (
        spread.reshape(members, fields_count, local_rows, width // TILE, TILE)
        * cell_factor[:, None, :, :, None]
    ).reshape(spread.shape)
    return (centre_fields[None] + scaled, factor)


def local(replica_variables, analysis, labels, pairing):
    size = lax.axis_size("lat")
    fields, local_rows, width = analysis.shape
    sub = width // TILE
    extent = local_rows + 2 * HALO
    planes = jax.ShapeDtypeStruct((fields, local_rows, sub, TILE), jnp.float32)
    edges = jax.ShapeDtypeStruct((2, sub, TILE), jnp.float32)
    label_planes = jnp.broadcast_to(labels.astype(jnp.float32)[..., None], (local_rows, sub, TILE))
    whole = pl.BlockSpec(memory_space=pltpu.VMEM)
    buffers = [
        pltpu.VMEM((fields * extent * sub, TILE), jnp.float32),
        pltpu.VMEM((extent * sub, TILE), jnp.float32),
    ]
    halo_sems = [pltpu.SemaphoreType.DMA((2, fields)), pltpu.SemaphoreType.DMA((2, fields))]
    first, edge = pl.pallas_call(
        functools.partial(first_kernel, size, local_rows, sub),
        out_shape=(planes, edges),
        in_specs=[whole] * 2,
        out_specs=(whole, whole),
        scratch_shapes=buffers + halo_sems + [pltpu.SemaphoreType.DMA((2,)), pltpu.SemaphoreType.DMA((2,))],
        compiler_params=pltpu.CompilerParams(collective_id=0, has_side_effects=True),
    )(replica_variables[0], label_planes)
    partner = partner_fields(first[None], pairing)[0]
    closing, factor = pl.pallas_call(
        functools.partial(second_kernel, size, local_rows, sub),
        out_shape=(
            jax.ShapeDtypeStruct(analysis.shape, jnp.float32),
            jax.ShapeDtypeStruct((1, REGIONS), jnp.float32),
        ),
        in_specs=[whole] * 5,
        out_specs=(whole, whole),
        scratch_shapes=buffers
        + [
            pltpu.VMEM((fields, local_rows, sub, TILE), jnp.float32),
            pltpu.VMEM((size, 2 * REGIONS, TILE), jnp.float32),
        ]
        + halo_sems
        + [pltpu.SemaphoreType.DMA((size,)), pltpu.SemaphoreType.DMA((size,))],
        compiler_params=pltpu.CompilerParams(collective_id=1, has_side_effects=True),
    )(first, partner, analysis, label_planes, edge)
    return (closing[None], factor)


def solution(mesh):
    return jax.shard_map(
        local,
        mesh=mesh,
        in_specs=(P("mem", None, "lat", None), P(None, "lat", None), P("lat", None), P()),
        out_specs=(P("mem", None, "lat", None), P("mem", None)),
        check_vma=False,
    )
```

```python
import functools

import jax
import numpy as np
import jax.numpy as jnp
from jax import lax
from jax.experimental import pallas as pl
from jax.experimental.pallas import tpu as pltpu
from jax.sharding import PartitionSpec as P

MESH = pl.DeviceIdType.MESH
TILE = 128
REGIONS = 8
STEPS = 3
HALO = 2 * STEPS
VMEM_LIMIT = 24 * 2**20
FIELDS = 4
REACH = (2 * STEPS - 1, 2 * STEPS - 1, 2 * STEPS, STEPS)


grav_coef = 0.1
depth_coef = 0.1
advect_coef = 0.05
diffuse_coef = 0.05
coriolis_coef = 0.05
target_size = 0.5
small_eps = 1e-06


def shift_lon(plane):
    sub = plane.shape[0]
    lane = lax.broadcasted_iota(jnp.int32, plane.shape, 1)
    east = pltpu.roll(plane, TILE - 1, 1)
    east = jnp.where(lane == TILE - 1, pltpu.roll(east, sub - 1, 0), east)
    west = pltpu.roll(plane, 1, 1)
    west = jnp.where(lane == 0, pltpu.roll(west, 1, 0), west)
    return east, west


def diff_lon(plane):
    east, west = shift_lon(plane)
    return east - west


def run_steps(state, buf, spare, local_rows, sub, start, rows_all):
    extent = local_rows + 2 * HALO

    def at(field, e):
        return pl.ds((field * extent + e) * sub, sub)

    def masked(e, plane):
        if HALO <= e < HALO + local_rows:
            return plane
        row = start + (e - HALO)
        return jnp.where((row >= 0) & (row < rows_all), 1.0, 0.0).astype(jnp.float32) * plane

    def coriolis(e):
        row = (start + (e - HALO)).astype(jnp.float32)
        return coriolis_coef * (2.0 * (row + 0.5) / rows_all - 1.0)

    tracer_source, source_field = state, 3
    for step in range(STEPS):
        margin = 2 * (STEPS - 1 - step)
        narrow = STEPS - 1 - step
        target, target_field = (spare, 0) if step % 2 == 0 else (buf, 3)
        own = (HALO, HALO + local_rows)
        for e in range(own[0] - margin - 1, own[1] + margin + 1):
            divergence = diff_lon(state[at(1, e), :]) + state[at(2, e + 1), :] - state[at(2, e - 1), :]
            buf[at(0, e), :] = masked(e, state[at(0, e), :] - depth_coef * divergence)
        for e in range(own[0] - margin, own[1] + margin):
            f = coriolis(e)
            v = state[at(2, e), :]
            u1 = state[at(1, e), :] + f * v - grav_coef * diff_lon(buf[at(0, e), :])
            slope = buf[at(0, e + 1), :] - buf[at(0, e - 1), :]
            buf[at(1, e), :] = u1
            buf[at(2, e), :] = masked(e, v - f * u1 - grav_coef * slope)
        for e in range(own[0] - narrow, own[1] + narrow):
            q = tracer_source[at(source_field, e), :]
            upper = tracer_source[at(source_field, e + 1), :]
            lower = tracer_source[at(source_field, e - 1), :]
            east, west = shift_lon(q)
            advected = buf[at(1, e), :] * (east - west) + buf[at(2, e), :] * (upper - lower)
            spreading = east + west + upper + lower - 4.0 * q
            target[at(target_field, e), :] = masked(e, q - advect_coef * advected + diffuse_coef * spreading)
        state = buf
        tracer_source, source_field = target, target_field
    return [(buf, 0), (buf, 1), (buf, 2), (tracer_source, source_field)]


def steps_kernel(size, local_rows, sub, as_rows, *refs):
    extent = local_rows + 2 * HALO
    if as_rows:
        state_ref, factor_ref, out_ref, factor_out, buf, spare = refs
        factor_out[...] = factor_ref[...]
    else:
        state_ref, out_ref, buf, spare = refs
    lat = lax.axis_index("lat")
    fields = run_steps(state_ref, buf, spare, local_rows, sub, lat * local_rows, local_rows * size)
    for field, (ref, place) in enumerate(fields):
        if not as_rows:
            out_ref[pl.ds(field * local_rows * sub, local_rows * sub), :] = ref[
                pl.ds((place * extent + HALO) * sub, local_rows * sub), :
            ]
            continue
        for row in range(0, local_rows, 8):
            for t in range(sub):
                first = (place * extent + HALO + row) * sub + t
                out_ref[field, row : row + 8, t * TILE : (t + 1) * TILE] = ref[pl.ds(first, 8, stride=sub), :]


def halo_copies(buf, local_rows, sub, lat, size, send_sem, recv_sem):
    extent = local_rows + 2 * HALO
    mem = lax.axis_index("mem")
    copies = []
    for side, peer in ((0, lat - 1), (1, lat + 1)):
        group = []
        for field in range(FIELDS):
            reach = REACH[field]
            source = HALO if side == 0 else HALO + local_rows - reach
            target = HALO + local_rows if side == 0 else HALO - reach
            group.append(
                pltpu.make_async_remote_copy(
                    src_ref=buf.at[pl.ds((field * extent + source) * sub, reach * sub), :],
                    dst_ref=buf.at[pl.ds((field * extent + target) * sub, reach * sub), :],
                    send_sem=send_sem.at[side, field],
                    recv_sem=recv_sem.at[side, field],
                    device_id=(mem, peer),
                    device_id_type=MESH,
                )
            )
        copies.append(group)
    return copies


def clear_outside(buf, local_rows, sub, lat, size):
    extent = local_rows + 2 * HALO
    zeros = jnp.zeros((HALO * sub, TILE), jnp.float32)

    @pl.when(lat == 0)
    def _():
        for field in range(FIELDS):
            buf[pl.ds(field * extent * sub, HALO * sub), :] = zeros

    @pl.when(lat == size - 1)
    def _():
        for field in range(FIELDS):
            buf[pl.ds((field * extent + HALO + local_rows) * sub, HALO * sub), :] = zeros


def start_halo(copies, lat, size):
    for side, has in ((0, lat > 0), (1, lat < size - 1)):

        @pl.when(has)
        def _(side=side):
            for copy in copies[side]:
                copy.start()


def finish_halo(copies, lat, size):
    for side, has in ((0, lat > 0), (1, lat < size - 1)):

        @pl.when(has)
        def _(side=side):
            for copy in copies[side]:
                copy.wait_send()
            for copy in copies[1 - side]:
                copy.wait_recv()


def planes_from_rows(source, buf, local_rows, sub):
    extent = local_rows + 2 * HALO
    for field in range(FIELDS):
        for row in range(0, local_rows, 8):
            for t in range(sub):
                first = (field * extent + HALO + row) * sub + t
                buf[pl.ds(first, 8, stride=sub), :] = source[field, row : row + 8, t * TILE : (t + 1) * TILE]


def first_kernel(size, local_rows, sub, x_ref, lab_ref, buf, edge_ref, send_sem, recv_sem, lab_send, lab_recv):
    lat = lax.axis_index("lat")
    mem = lax.axis_index("mem")
    barrier = pltpu.get_barrier_semaphore()
    for peer, has in ((lat - 1, lat > 0), (lat + 1, lat < size - 1)):

        @pl.when(has)
        def _(peer=peer):
            pl.semaphore_signal(barrier, inc=1, device_id=(mem, peer), device_id_type=MESH)

    clear_outside(buf, local_rows, sub, lat, size)
    planes_from_rows(x_ref, buf, local_rows, sub)
    none = jnp.full((sub, TILE), -1.0, jnp.float32)

    @pl.when(lat == 0)
    def _():
        edge_ref[0] = none

    @pl.when(lat == size - 1)
    def _():
        edge_ref[1] = none

    inner = (lat > 0) & (lat < size - 1)

    @pl.when(inner)
    def _():
        pl.semaphore_wait(barrier, 2)

    @pl.when(jnp.logical_not(inner))
    def _():
        pl.semaphore_wait(barrier, 1)

    copies = halo_copies(buf, local_rows, sub, lat, size, send_sem, recv_sem)
    for side, peer in ((0, lat - 1), (1, lat + 1)):
        row = 0 if side == 0 else local_rows - 1
        copies[side].append(
            pltpu.make_async_remote_copy(
                src_ref=lab_ref.at[row],
                dst_ref=edge_ref.at[1 - side],
                send_sem=lab_send.at[side],
                recv_sem=lab_recv.at[side],
                device_id=(mem, peer),
                device_id_type=MESH,
            )
        )
    start_halo(copies, lat, size)
    finish_halo(copies, lat, size)


def second_kernel(
    size, local_rows, sub, first_ref, partner_ref, analysis_ref, lab_ref, edge_ref, buf, factor_ref,
    spread, sums, send_sem, recv_sem, sum_send, sum_recv,
):
    lat = lax.axis_index("lat")
    mem = lax.axis_index("mem")
    extent = local_rows + 2 * HALO
    barrier = pltpu.get_barrier_semaphore()
    for hop in range(1, size):
        pl.semaphore_signal(barrier, inc=1, device_id=(mem, lax.rem(lat + hop, size)), device_id_type=MESH)

    def fold(plane):
        total = plane[0:8]
        for i in range(8, sub, 8):
            total = total + plane[i : i + 8]
        return total

    energies = [jnp.zeros((8, TILE), jnp.float32) for _ in range(REGIONS)]
    counts = [jnp.zeros((8, TILE), jnp.float32) for _ in range(REGIONS)]

    def accumulate(row, carry):
        energies, counts = carry
        total = jnp.zeros((sub, TILE), jnp.float32)
        for field in range(FIELDS):
            place = pl.ds(pl.multiple_of((field * local_rows + row) * sub, sub), sub)
            half = 0.5 * (first_ref[place, :] - partner_ref[place, :])
            spread[field, row] = half
            total = total + half * half
        quarter = 0.125 * total
        here = lab_ref[row]
        before = jnp.where(row == 0, edge_ref[0], lab_ref[jnp.maximum(row - 1, 0)])
        after = jnp.where(row == local_rows - 1, edge_ref[1], lab_ref[jnp.minimum(row + 1, local_rows - 1)])
        new_energies, new_counts = [], []
        for k in range(REGIONS):
            kept = jnp.where(here == k, 1.0, 0.0)
            weight = 2.0 * kept + jnp.where(before == k, 1.0, 0.0) + jnp.where(after == k, 1.0, 0.0)
            new_energies.append(energies[k] + fold(quarter * weight))
            new_counts.append(counts[k] + fold(kept))
        return new_energies, new_counts

    energies, counts = lax.fori_loop(0, local_rows, accumulate, (energies, counts))
    for k in range(REGIONS):
        sums[0, k : k + 1, :] = jnp.sum(energies[k], axis=0, keepdims=True)
        sums[0, REGIONS + k : REGIONS + k + 1, :] = jnp.sum(counts[k], axis=0, keepdims=True)

    pl.semaphore_wait(barrier, size - 1)
    sends = []
    for hop in range(1, size):
        sends.append(
            pltpu.make_async_remote_copy(
                src_ref=sums.at[0],
                dst_ref=sums.at[hop],
                send_sem=sum_send.at[hop],
                recv_sem=sum_recv.at[hop],
                device_id=(mem, lax.rem(lat + hop, size)),
                device_id_type=MESH,
            )
        )
    for copy in sends:
        copy.start()
    clear_outside(buf, local_rows, sub, lat, size)
    planes_from_rows(analysis_ref, buf, local_rows, sub)
    for copy in sends:
        copy.wait()
    total = sums[0]
    for hop in range(1, size):
        total = total + sums[hop]
    total = jnp.sum(total, axis=1, keepdims=True)
    factor = target_size / jnp.sqrt(total[:REGIONS] / total[REGIONS:] + small_eps)
    wide = jnp.broadcast_to(factor, (REGIONS, TILE))
    diagonal = lax.broadcasted_iota(jnp.int32, (REGIONS, TILE), 0) == lax.broadcasted_iota(
        jnp.int32, (REGIONS, TILE), 1
    )
    factor_ref[...] = jnp.sum(jnp.where(diagonal, wide, 0.0), axis=0, keepdims=True)[:, :REGIONS]
    lanes = [jnp.broadcast_to(wide[k : k + 1], (sub, TILE)) for k in range(REGIONS)]

    def middle(row, carry):
        here = lab_ref[row]
        scale = lanes[0]
        for k in range(1, REGIONS):
            scale = jnp.where(here == k, lanes[k], scale)
        for field in range(FIELDS):
            place = pl.ds(pl.multiple_of((field * extent + HALO + row) * sub, sub), sub)
            buf[place, :] = buf[place, :] + scale * spread[field, row]
        return carry

    lax.fori_loop(0, local_rows, middle, 0)
    copies = halo_copies(buf, local_rows, sub, lat, size, send_sem, recv_sem)
    start_halo(copies, lat, size)
    finish_halo(copies, lat, size)


def matchings(items):
    if not items:
        return [[]]
    first, rest = items[0], items[1:]
    return [
        [(first, other)] + tail
        for i, other in enumerate(rest)
        for tail in matchings(rest[:i] + rest[i + 1 :])
    ]


def matchings_count(size):
    count = 1
    for i in range(size - 1, 0, -2):
        count *= i
    return count


def partner_fields(fields, pairing):
    size = lax.axis_size("mem")
    if matchings_count(size) > 512:
        piece = lax.all_gather(fields, "mem", axis=0)
        partner_index = pairing[lax.axis_index("mem")]
        return lax.dynamic_index_in_dim(piece, partner_index, 0, keepdims=False)
    perms = [
        [(i, j) for i, j in match] + [(j, i) for i, j in match]
        for match in matchings(list(range(size)))
    ]
    table = np.zeros((len(perms), size), np.int32)
    for row, perm in enumerate(perms):
        for i, j in perm:
            table[row, i] = j
    hits = jnp.all(jnp.asarray(table) == pairing[None], axis=1)
    index = jnp.sum(jnp.where(hits, jnp.arange(len(perms), dtype=jnp.int32), 0))
    branches = [functools.partial(lax.ppermute, axis_name="mem", perm=perm) for perm in perms]
    return lax.switch(index, branches, fields)


def recentre(spread, centre_fields, region_sum, cells, onehot):
    factor = target_size / jnp.sqrt(region_sum / cells + small_eps)
    cell_factor = jnp.einsum("mk,rtk->mrt", factor, onehot, precision=lax.Precision.HIGHEST)
    members, fields_count, local_rows, width = spread.shape
    scaled = (
        spread.reshape(members, fields_count, local_rows, width // TILE, TILE)
        * cell_factor[:, None, :, :, None]
    ).reshape(spread.shape)
    return (centre_fields[None] + scaled, factor)


def local(replica_variables, analysis, labels, pairing):
    size = lax.axis_size("lat")
    fields, local_rows, width = analysis.shape
    sub = width // TILE
    extent = local_rows + 2 * HALO
    planes = jax.ShapeDtypeStruct((fields * local_rows * sub, TILE), jnp.float32)
    extended = jax.ShapeDtypeStruct((fields * extent * sub, TILE), jnp.float32)
    edges = jax.ShapeDtypeStruct((2, sub, TILE), jnp.float32)
    factors = jax.ShapeDtypeStruct((1, REGIONS), jnp.float32)
    label_planes = jnp.broadcast_to(labels.astype(jnp.float32)[..., None], (local_rows, sub, TILE))
    whole = pl.BlockSpec(memory_space=pltpu.VMEM)
    buffers = [
        pltpu.VMEM((fields * extent * sub, TILE), jnp.float32),
        pltpu.VMEM((extent * sub, TILE), jnp.float32),
    ]
    halo_sems = [pltpu.SemaphoreType.DMA((2, fields)), pltpu.SemaphoreType.DMA((2, fields))]
    state, edge = pl.pallas_call(
        functools.partial(first_kernel, size, local_rows, sub),
        out_shape=(extended, edges),
        in_specs=[whole] * 2,
        out_specs=(whole, whole),
        scratch_shapes=halo_sems + [pltpu.SemaphoreType.DMA((2,)), pltpu.SemaphoreType.DMA((2,))],
        compiler_params=pltpu.CompilerParams(collective_id=0, has_side_effects=True, vmem_limit_bytes=VMEM_LIMIT),
    )(replica_variables[0], label_planes)
    first = pl.pallas_call(
        functools.partial(steps_kernel, size, local_rows, sub, False),
        out_shape=planes,
        in_specs=[whole],
        out_specs=whole,
        scratch_shapes=buffers,
        compiler_params=pltpu.CompilerParams(vmem_limit_bytes=VMEM_LIMIT),
    )(state)
    partner = partner_fields(first, pairing)
    state, factor = pl.pallas_call(
        functools.partial(second_kernel, size, local_rows, sub),
        out_shape=(extended, factors),
        in_specs=[whole] * 5,
        out_specs=(whole, whole),
        scratch_shapes=[
            pltpu.VMEM((fields, local_rows, sub, TILE), jnp.float32),
            pltpu.VMEM((size, 2 * REGIONS, TILE), jnp.float32),
        ]
        + halo_sems
        + [pltpu.SemaphoreType.DMA((size,)), pltpu.SemaphoreType.DMA((size,))],
        compiler_params=pltpu.CompilerParams(collective_id=1, has_side_effects=True, vmem_limit_bytes=VMEM_LIMIT),
    )(first, partner, analysis, label_planes, edge)
    closing, factor = pl.pallas_call(
        functools.partial(steps_kernel, size, local_rows, sub, True),
        out_shape=(jax.ShapeDtypeStruct(analysis.shape, jnp.float32), factors),
        in_specs=[whole] * 2,
        out_specs=(whole, whole),
        scratch_shapes=buffers,
        compiler_params=pltpu.CompilerParams(vmem_limit_bytes=VMEM_LIMIT),
    )(state, factor)
    return (closing[None], factor)


def solution(mesh):
    return jax.shard_map(
        local,
        mesh=mesh,
        in_specs=(P("mem", None, "lat", None), P(None, "lat", None), P("lat", None), P()),
        out_specs=(P("mem", None, "lat", None), P("mem", None)),
        check_vma=False,
    )
```

```python
import functools

import jax
import jax.numpy as jnp
from jax import lax
from jax.experimental import pallas as pl
from jax.experimental.pallas import tpu as pltpu
from jax.sharding import PartitionSpec as P

MESH = pl.DeviceIdType.MESH
TILE = 128
REGIONS = 8
STEPS = 3
HALO = 2 * STEPS
VMEM_LIMIT = 24 * 2**20
FIELDS = 4
REACH = (2 * STEPS - 1, 2 * STEPS - 1, 2 * STEPS, STEPS)


grav_coef = 0.1
depth_coef = 0.1
advect_coef = 0.05
diffuse_coef = 0.05
coriolis_coef = 0.05
target_size = 0.5
small_eps = 1e-06


def shift_lon(plane):
    sub = plane.shape[0]
    lane = lax.broadcasted_iota(jnp.int32, plane.shape, 1)
    east = pltpu.roll(plane, TILE - 1, 1)
    east = jnp.where(lane == TILE - 1, pltpu.roll(east, sub - 1, 0), east)
    west = pltpu.roll(plane, 1, 1)
    west = jnp.where(lane == 0, pltpu.roll(west, 1, 0), west)
    return east, west


def diff_lon(plane):
    east, west = shift_lon(plane)
    return east - west


def run_steps(state, buf, spare, local_rows, sub, start, rows_all):
    extent = local_rows + 2 * HALO

    def at(field, e):
        return pl.ds((field * extent + e) * sub, sub)

    def masked(e, plane):
        if HALO <= e < HALO + local_rows:
            return plane
        row = start + (e - HALO)
        return jnp.where((row >= 0) & (row < rows_all), 1.0, 0.0).astype(jnp.float32) * plane

    def coriolis(e):
        row = (start + (e - HALO)).astype(jnp.float32)
        return coriolis_coef * (2.0 * (row + 0.5) / rows_all - 1.0)

    tracer_source, source_field = state, 3
    for step in range(STEPS):
        margin = 2 * (STEPS - 1 - step)
        narrow = STEPS - 1 - step
        target, target_field = (spare, 0) if step % 2 == 0 else (buf, 3)
        own = (HALO, HALO + local_rows)
        for e in range(own[0] - margin - 1, own[1] + margin + 1):
            divergence = diff_lon(state[at(1, e), :]) + state[at(2, e + 1), :] - state[at(2, e - 1), :]
            buf[at(0, e), :] = masked(e, state[at(0, e), :] - depth_coef * divergence)
        for e in range(own[0] - margin, own[1] + margin):
            f = coriolis(e)
            v = state[at(2, e), :]
            u1 = state[at(1, e), :] + f * v - grav_coef * diff_lon(buf[at(0, e), :])
            slope = buf[at(0, e + 1), :] - buf[at(0, e - 1), :]
            buf[at(1, e), :] = u1
            buf[at(2, e), :] = masked(e, v - f * u1 - grav_coef * slope)
        for e in range(own[0] - narrow, own[1] + narrow):
            q = tracer_source[at(source_field, e), :]
            upper = tracer_source[at(source_field, e + 1), :]
            lower = tracer_source[at(source_field, e - 1), :]
            east, west = shift_lon(q)
            advected = buf[at(1, e), :] * (east - west) + buf[at(2, e), :] * (upper - lower)
            spreading = east + west + upper + lower - 4.0 * q
            target[at(target_field, e), :] = masked(e, q - advect_coef * advected + diffuse_coef * spreading)
        state = buf
        tracer_source, source_field = target, target_field
    return [(buf, 0), (buf, 1), (buf, 2), (tracer_source, source_field)]


def matchings(items):
    if not items:
        return [[]]
    first, rest = items[0], items[1:]
    return [
        [(first, other)] + tail
        for i, other in enumerate(rest)
        for tail in matchings(rest[:i] + rest[i + 1 :])
    ]


def permutations(size):
    count = 1
    for i in range(size - 1, 0, -2):
        count *= i
    if count > 512:
        return []
    return [[(i, j) for i, j in m] + [(j, i) for i, j in m] for m in matchings(list(range(size)))]


def matching_index(pairing_ref):
    size = pairing_ref.shape[0]
    key = 0
    for i in range(size):
        key = key * size + pairing_ref[i]
    index = jnp.int32(0)
    for branch, perm in enumerate(permutations(size)):
        known = 0
        for _, j in sorted(perm):
            known = known * size + j
        index = jnp.where(key == known, branch, index)
    return index


def steps_kernel(size, local_rows, sub, as_rows, *refs):
    extent = local_rows + 2 * HALO
    if as_rows:
        state_ref, factor_ref, out_ref, factor_out, buf, spare = refs
        factor_out[...] = factor_ref[...]
    else:
        state_ref, pairing_ref, out_ref, index_ref, buf, spare = refs
        index_ref[0, 0] = matching_index(pairing_ref)
    lat = lax.axis_index("lat")
    fields = run_steps(state_ref, buf, spare, local_rows, sub, lat * local_rows, local_rows * size)
    for field, (ref, place) in enumerate(fields):
        if not as_rows:
            for tile in range(local_rows * sub // 8):
                column = (field * local_rows * sub // 8 + tile) * TILE
                out_ref[:, column : column + TILE] = ref[pl.ds((place * extent + HALO) * sub + tile * 8, 8), :]
            continue
        for row in range(0, local_rows, 8):
            for t in range(sub):
                first = (place * extent + HALO + row) * sub + t
                out_ref[field, row : row + 8, t * TILE : (t + 1) * TILE] = ref[pl.ds(first, 8, stride=sub), :]


def halo_copies(buf, local_rows, sub, lat, size, send_sem, recv_sem):
    extent = local_rows + 2 * HALO
    mem = lax.axis_index("mem")
    copies = []
    for side, peer in ((0, lat - 1), (1, lat + 1)):
        group = []
        for field in range(FIELDS):
            reach = REACH[field]
            source = HALO if side == 0 else HALO + local_rows - reach
            target = HALO + local_rows if side == 0 else HALO - reach
            group.append(
                pltpu.make_async_remote_copy(
                    src_ref=buf.at[pl.ds((field * extent + source) * sub, reach * sub), :],
                    dst_ref=buf.at[pl.ds((field * extent + target) * sub, reach * sub), :],
                    send_sem=send_sem.at[side, field],
                    recv_sem=recv_sem.at[side, field],
                    device_id=(mem, peer),
                    device_id_type=MESH,
                )
            )
        copies.append(group)
    return copies


def clear_outside(buf, local_rows, sub, lat, size):
    extent = local_rows + 2 * HALO
    zeros = jnp.zeros((HALO * sub, TILE), jnp.float32)

    @pl.when(lat == 0)
    def _():
        for field in range(FIELDS):
            buf[pl.ds(field * extent * sub, HALO * sub), :] = zeros

    @pl.when(lat == size - 1)
    def _():
        for field in range(FIELDS):
            buf[pl.ds((field * extent + HALO + local_rows) * sub, HALO * sub), :] = zeros


def start_halo(copies, lat, size):
    for side, has in ((0, lat > 0), (1, lat < size - 1)):

        @pl.when(has)
        def _(side=side):
            for copy in copies[side]:
                copy.start()


def finish_halo(copies, lat, size):
    for side, has in ((0, lat > 0), (1, lat < size - 1)):

        @pl.when(has)
        def _(side=side):
            for copy in copies[side]:
                copy.wait_send()
            for copy in copies[1 - side]:
                copy.wait_recv()


def planes_from_rows(source, buf, local_rows, sub, fields=range(FIELDS)):
    extent = local_rows + 2 * HALO
    for field in fields:
        for row in range(0, local_rows, 8):
            for t in range(sub):
                first = (field * extent + HALO + row) * sub + t
                buf[pl.ds(first, 8, stride=sub), :] = source[field, row : row + 8, t * TILE : (t + 1) * TILE]


def first_kernel(size, local_rows, sub, x_ref, lab_ref, buf, edge_ref, rows, load_sem, send_sem, recv_sem, lab_send, lab_recv):
    lat = lax.axis_index("lat")
    mem = lax.axis_index("mem")
    barrier = pltpu.get_barrier_semaphore()
    for peer, has in ((lat - 1, lat > 0), (lat + 1, lat < size - 1)):

        @pl.when(has)
        def _(peer=peer):
            pl.semaphore_signal(barrier, inc=1, device_id=(mem, peer), device_id_type=MESH)

    loads = [pltpu.make_async_copy(x_ref.at[f], rows.at[f], load_sem.at[f]) for f in range(FIELDS)]
    for load in loads:
        load.start()
    clear_outside(buf, local_rows, sub, lat, size)
    none = jnp.full((sub, TILE), -1.0, jnp.float32)

    @pl.when(lat == 0)
    def _():
        edge_ref[0] = none

    @pl.when(lat == size - 1)
    def _():
        edge_ref[1] = none

    inner = (lat > 0) & (lat < size - 1)

    @pl.when(inner)
    def _():
        pl.semaphore_wait(barrier, 2)

    @pl.when(jnp.logical_not(inner))
    def _():
        pl.semaphore_wait(barrier, 1)

    copies = halo_copies(buf, local_rows, sub, lat, size, send_sem, recv_sem)
    for side, peer in ((0, lat - 1), (1, lat + 1)):
        row = 0 if side == 0 else local_rows - 1
        copies[side].append(
            pltpu.make_async_remote_copy(
                src_ref=lab_ref.at[row],
                dst_ref=edge_ref.at[1 - side],
                send_sem=lab_send.at[side],
                recv_sem=lab_recv.at[side],
                device_id=(mem, peer),
                device_id_type=MESH,
            )
        )
    for field in range(FIELDS + 1):
        if field < FIELDS:
            loads[field].wait()
            planes_from_rows(rows, buf, local_rows, sub, (field,))
        start_halo([side[field : field + 1] for side in copies], lat, size)
    finish_halo(copies, lat, size)


def second_kernel(
    size, local_rows, sub, first_ref, partner_ref, analysis_ref, lab_ref, edge_ref, buf, factor_ref,
    spread, sums, send_sem, recv_sem, sum_send, sum_recv,
):
    lat = lax.axis_index("lat")
    mem = lax.axis_index("mem")
    extent = local_rows + 2 * HALO
    barrier = pltpu.get_barrier_semaphore()
    for hop in range(1, size):
        pl.semaphore_signal(barrier, inc=1, device_id=(mem, lax.rem(lat + hop, size)), device_id_type=MESH)

    def fold(plane):
        total = plane[0:8]
        for i in range(8, sub, 8):
            total = total + plane[i : i + 8]
        return total

    energies = [jnp.zeros((8, TILE), jnp.float32) for _ in range(REGIONS)]
    counts = [jnp.zeros((8, TILE), jnp.float32) for _ in range(REGIONS)]

    def accumulate(row, carry):
        energies, counts = carry
        total = jnp.zeros((sub, TILE), jnp.float32)
        for field in range(FIELDS):
            parts = []
            for i in range(sub // 8):
                column = ((field * local_rows + row) * (sub // 8) + i) * TILE
                place = pl.ds(pl.multiple_of(column, TILE), TILE)
                parts.append(first_ref[:, place] - partner_ref[:, place])
            half = 0.5 * jnp.concatenate(parts, axis=0)
            spread[field, row] = half
            total = total + half * half
        quarter = 0.125 * total
        here = lab_ref[row]
        before = jnp.where(row == 0, edge_ref[0], lab_ref[jnp.maximum(row - 1, 0)])
        after = jnp.where(row == local_rows - 1, edge_ref[1], lab_ref[jnp.minimum(row + 1, local_rows - 1)])
        new_energies, new_counts = [], []
        for k in range(REGIONS):
            kept = jnp.where(here == k, 1.0, 0.0)
            weight = 2.0 * kept + jnp.where(before == k, 1.0, 0.0) + jnp.where(after == k, 1.0, 0.0)
            new_energies.append(energies[k] + fold(quarter * weight))
            new_counts.append(counts[k] + fold(kept))
        return new_energies, new_counts

    energies, counts = lax.fori_loop(0, local_rows, accumulate, (energies, counts))
    for k in range(REGIONS):
        sums[0, k : k + 1, :] = jnp.sum(energies[k], axis=0, keepdims=True)
        sums[0, REGIONS + k : REGIONS + k + 1, :] = jnp.sum(counts[k], axis=0, keepdims=True)

    pl.semaphore_wait(barrier, size - 1)
    sends = []
    for hop in range(1, size):
        sends.append(
            pltpu.make_async_remote_copy(
                src_ref=sums.at[0],
                dst_ref=sums.at[hop],
                send_sem=sum_send.at[hop],
                recv_sem=sum_recv.at[hop],
                device_id=(mem, lax.rem(lat + hop, size)),
                device_id_type=MESH,
            )
        )
    for copy in sends:
        copy.start()
    clear_outside(buf, local_rows, sub, lat, size)
    planes_from_rows(analysis_ref, buf, local_rows, sub)
    for copy in sends:
        copy.wait()
    total = sums[0]
    for hop in range(1, size):
        total = total + sums[hop]
    total = jnp.sum(total, axis=1, keepdims=True)
    factor = target_size / jnp.sqrt(total[:REGIONS] / total[REGIONS:] + small_eps)
    wide = jnp.broadcast_to(factor, (REGIONS, TILE))
    diagonal = lax.broadcasted_iota(jnp.int32, (REGIONS, TILE), 0) == lax.broadcasted_iota(
        jnp.int32, (REGIONS, TILE), 1
    )
    factor_ref[...] = jnp.sum(jnp.where(diagonal, wide, 0.0), axis=0, keepdims=True)[:, :REGIONS]
    lanes = [jnp.broadcast_to(wide[k : k + 1], (sub, TILE)) for k in range(REGIONS)]

    def middle(row, carry):
        here = lab_ref[row]
        scale = lanes[0]
        for k in range(1, REGIONS):
            scale = jnp.where(here == k, lanes[k], scale)
        for field in range(FIELDS):
            place = pl.ds(pl.multiple_of((field * extent + HALO + row) * sub, sub), sub)
            buf[place, :] = buf[place, :] + scale * spread[field, row]
        return carry

    lax.fori_loop(0, local_rows, middle, 0)
    copies = halo_copies(buf, local_rows, sub, lat, size, send_sem, recv_sem)
    start_halo(copies, lat, size)
    finish_halo(copies, lat, size)


def partner_fields(fields, pairing, index):
    size = lax.axis_size("mem")
    perms = permutations(size)
    if not perms:
        piece = lax.all_gather(fields, "mem", axis=0)
        return lax.dynamic_index_in_dim(piece, pairing[lax.axis_index("mem")], 0, keepdims=False)
    branches = [functools.partial(lax.ppermute, axis_name="mem", perm=perm) for perm in perms]
    return lax.switch(index, branches, fields)


def local(replica_variables, analysis, labels, pairing):
    size = lax.axis_size("lat")
    fields, local_rows, width = analysis.shape
    sub = width // TILE
    extent = local_rows + 2 * HALO
    wide = jax.ShapeDtypeStruct((8, fields * local_rows * width // 8), jnp.float32)
    extended = jax.ShapeDtypeStruct((fields * extent * sub, TILE), jnp.float32)
    edges = jax.ShapeDtypeStruct((2, sub, TILE), jnp.float32)
    factors = jax.ShapeDtypeStruct((1, REGIONS), jnp.float32)
    label_planes = jnp.broadcast_to(labels.astype(jnp.float32)[..., None], (local_rows, sub, TILE))
    whole = pl.BlockSpec(memory_space=pltpu.VMEM)
    buffers = [
        pltpu.VMEM((fields * extent * sub, TILE), jnp.float32),
        pltpu.VMEM((extent * sub, TILE), jnp.float32),
    ]
    halo_sems = [pltpu.SemaphoreType.DMA((2, fields)), pltpu.SemaphoreType.DMA((2, fields))]
    state, edge = pl.pallas_call(
        functools.partial(first_kernel, size, local_rows, sub),
        out_shape=(extended, edges),
        in_specs=[pl.BlockSpec(memory_space=pltpu.HBM), whole],
        out_specs=(whole, whole),
        scratch_shapes=[pltpu.VMEM(analysis.shape, jnp.float32), pltpu.SemaphoreType.DMA((fields,))]
        + halo_sems
        + [pltpu.SemaphoreType.DMA((2,)), pltpu.SemaphoreType.DMA((2,))],
        compiler_params=pltpu.CompilerParams(collective_id=0, has_side_effects=True, vmem_limit_bytes=VMEM_LIMIT),
    )(replica_variables[0], label_planes)
    smem = pl.BlockSpec(memory_space=pltpu.SMEM)
    first, index = pl.pallas_call(
        functools.partial(steps_kernel, size, local_rows, sub, False),
        out_shape=(wide, jax.ShapeDtypeStruct((1, 1), jnp.int32)),
        in_specs=[whole, smem],
        out_specs=(whole, smem),
        scratch_shapes=buffers,
        compiler_params=pltpu.CompilerParams(vmem_limit_bytes=VMEM_LIMIT),
    )(state, pairing)
    partner = partner_fields(first, pairing, index[0, 0])
    state, factor = pl.pallas_call(
        functools.partial(second_kernel, size, local_rows, sub),
        out_shape=(extended, factors),
        in_specs=[whole] * 5,
        out_specs=(whole, whole),
        scratch_shapes=[
            pltpu.VMEM((fields, local_rows, sub, TILE), jnp.float32),
            pltpu.VMEM((size, 2 * REGIONS, TILE), jnp.float32),
        ]
        + halo_sems
        + [pltpu.SemaphoreType.DMA((size,)), pltpu.SemaphoreType.DMA((size,))],
        compiler_params=pltpu.CompilerParams(collective_id=1, has_side_effects=True, vmem_limit_bytes=VMEM_LIMIT),
    )(first, partner, analysis, label_planes, edge)
    closing, factor = pl.pallas_call(
        functools.partial(steps_kernel, size, local_rows, sub, True),
        out_shape=(jax.ShapeDtypeStruct(analysis.shape, jnp.float32), factors),
        in_specs=[whole] * 2,
        out_specs=(whole, whole),
        scratch_shapes=buffers,
        compiler_params=pltpu.CompilerParams(vmem_limit_bytes=VMEM_LIMIT),
    )(state, factor)
    return (closing[None], factor)


def solution(mesh):
    return jax.shard_map(
        local,
        mesh=mesh,
        in_specs=(P("mem", None, "lat", None), P(None, "lat", None), P("lat", None), P()),
        out_specs=(P("mem", None, "lat", None), P("mem", None)),
        check_vma=False,
    )
```

```python
import functools

import jax
import jax.numpy as jnp
from jax import lax
from jax.experimental import pallas as pl
from jax.experimental.pallas import tpu as pltpu
from jax.sharding import PartitionSpec as P

MESH = pl.DeviceIdType.MESH
TILE = 128
REGIONS = 8
STEPS = 3
MAX_BRANCHES = 28
HALO = 2 * STEPS
VMEM_LIMIT = 24 * 2**20
FIELDS = 4
REACH = (2 * STEPS - 1, 2 * STEPS - 1, 2 * STEPS, STEPS)


grav_coef = 0.1
depth_coef = 0.1
advect_coef = 0.05
diffuse_coef = 0.05
coriolis_coef = 0.05
target_size = 0.5
small_eps = 1e-06


def shift_lon(plane):
    sub = plane.shape[0]
    lane = lax.broadcasted_iota(jnp.int32, plane.shape, 1)
    east = pltpu.roll(plane, TILE - 1, 1)
    east = jnp.where(lane == TILE - 1, pltpu.roll(east, sub - 1, 0), east)
    west = pltpu.roll(plane, 1, 1)
    west = jnp.where(lane == 0, pltpu.roll(west, 1, 0), west)
    return east, west


def diff_lon(plane):
    east, west = shift_lon(plane)
    return east - west


def run_steps(state, buf, spare, local_rows, sub, start, rows_all):
    extent = local_rows + 2 * HALO

    def at(field, e):
        return pl.ds((field * extent + e) * sub, sub)

    def masked(e, plane):
        if HALO <= e < HALO + local_rows:
            return plane
        row = start + (e - HALO)
        return jnp.where((row >= 0) & (row < rows_all), 1.0, 0.0).astype(jnp.float32) * plane

    def coriolis(e):
        row = (start + (e - HALO)).astype(jnp.float32)
        return coriolis_coef * (2.0 * (row + 0.5) / rows_all - 1.0)

    tracer_source, source_field = state, 3
    for step in range(STEPS):
        margin = 2 * (STEPS - 1 - step)
        narrow = STEPS - 1 - step
        target, target_field = (spare, 0) if step % 2 == 0 else (buf, 3)
        own = (HALO, HALO + local_rows)
        for e in range(own[0] - margin - 1, own[1] + margin + 1):
            divergence = diff_lon(state[at(1, e), :]) + state[at(2, e + 1), :] - state[at(2, e - 1), :]
            buf[at(0, e), :] = masked(e, state[at(0, e), :] - depth_coef * divergence)
        for e in range(own[0] - margin, own[1] + margin):
            f = coriolis(e)
            v = state[at(2, e), :]
            u1 = state[at(1, e), :] + f * v - grav_coef * diff_lon(buf[at(0, e), :])
            slope = buf[at(0, e + 1), :] - buf[at(0, e - 1), :]
            buf[at(1, e), :] = u1
            buf[at(2, e), :] = masked(e, v - f * u1 - grav_coef * slope)
        for e in range(own[0] - narrow, own[1] + narrow):
            q = tracer_source[at(source_field, e), :]
            upper = tracer_source[at(source_field, e + 1), :]
            lower = tracer_source[at(source_field, e - 1), :]
            east, west = shift_lon(q)
            advected = buf[at(1, e), :] * (east - west) + buf[at(2, e), :] * (upper - lower)
            spreading = east + west + upper + lower - 4.0 * q
            target[at(target_field, e), :] = masked(e, q - advect_coef * advected + diffuse_coef * spreading)
        state = buf
        tracer_source, source_field = target, target_field
    return [(buf, 0), (buf, 1), (buf, 2), (tracer_source, source_field)]


def pairs_of(size):
    return [(a, b) for a in range(size) for b in range(a + 1, size)]


def pair_index(pairing_ref):
    size = pairing_ref.shape[0]
    me = lax.axis_index("mem")
    partner = pairing_ref[me]
    low, high = jnp.minimum(me, partner), jnp.maximum(me, partner)
    return low * (2 * size - low - 1) // 2 + high - low - 1


def steps_kernel(size, local_rows, sub, as_rows, *refs):
    extent = local_rows + 2 * HALO
    if as_rows:
        state_ref, factor_ref, out_ref, factor_out, buf, spare = refs
        factor_out[...] = factor_ref[...]
    else:
        state_ref, pairing_ref, out_ref, index_ref, buf, spare = refs
        index_ref[0, 0] = pair_index(pairing_ref)
    lat = lax.axis_index("lat")
    fields = run_steps(state_ref, buf, spare, local_rows, sub, lat * local_rows, local_rows * size)
    for field, (ref, place) in enumerate(fields):
        if not as_rows:
            for tile in range(local_rows * sub // 8):
                column = (field * local_rows * sub // 8 + tile) * TILE
                out_ref[:, column : column + TILE] = ref[pl.ds((place * extent + HALO) * sub + tile * 8, 8), :]
            continue
        for row in range(0, local_rows, 8):
            for t in range(sub):
                first = (place * extent + HALO + row) * sub + t
                out_ref[field, row : row + 8, t * TILE : (t + 1) * TILE] = ref[pl.ds(first, 8, stride=sub), :]


def halo_copies(buf, local_rows, sub, lat, size, send_sem, recv_sem):
    extent = local_rows + 2 * HALO
    mem = lax.axis_index("mem")
    copies = []
    for side, peer in ((0, lat - 1), (1, lat + 1)):
        group = []
        for field in range(FIELDS):
            reach = REACH[field]
            source = HALO if side == 0 else HALO + local_rows - reach
            target = HALO + local_rows if side == 0 else HALO - reach
            group.append(
                pltpu.make_async_remote_copy(
                    src_ref=buf.at[pl.ds((field * extent + source) * sub, reach * sub), :],
                    dst_ref=buf.at[pl.ds((field * extent + target) * sub, reach * sub), :],
                    send_sem=send_sem.at[side, field],
                    recv_sem=recv_sem.at[side, field],
                    device_id=(mem, peer),
                    device_id_type=MESH,
                )
            )
        copies.append(group)
    return copies


def clear_outside(buf, local_rows, sub, lat, size):
    extent = local_rows + 2 * HALO
    zeros = jnp.zeros((HALO * sub, TILE), jnp.float32)

    @pl.when(lat == 0)
    def _():
        for field in range(FIELDS):
            buf[pl.ds(field * extent * sub, HALO * sub), :] = zeros

    @pl.when(lat == size - 1)
    def _():
        for field in range(FIELDS):
            buf[pl.ds((field * extent + HALO + local_rows) * sub, HALO * sub), :] = zeros


def start_halo(copies, lat, size):
    for side, has in ((0, lat > 0), (1, lat < size - 1)):

        @pl.when(has)
        def _(side=side):
            for copy in copies[side]:
                copy.start()


def finish_halo(copies, lat, size):
    for side, has in ((0, lat > 0), (1, lat < size - 1)):

        @pl.when(has)
        def _(side=side):
            for copy in copies[side]:
                copy.wait_send()
            for copy in copies[1 - side]:
                copy.wait_recv()


def planes_from_rows(source, buf, local_rows, sub, fields=range(FIELDS)):
    extent = local_rows + 2 * HALO
    for field in fields:
        for row in range(0, local_rows, 8):
            for t in range(sub):
                first = (field * extent + HALO + row) * sub + t
                buf[pl.ds(first, 8, stride=sub), :] = source[field, row : row + 8, t * TILE : (t + 1) * TILE]


def first_kernel(size, local_rows, sub, x_ref, lab_ref, buf, edge_ref, rows, load_sem, send_sem, recv_sem, lab_send, lab_recv):
    lat = lax.axis_index("lat")
    mem = lax.axis_index("mem")
    barrier = pltpu.get_barrier_semaphore()
    for peer, has in ((lat - 1, lat > 0), (lat + 1, lat < size - 1)):

        @pl.when(has)
        def _(peer=peer):
            pl.semaphore_signal(barrier, inc=1, device_id=(mem, peer), device_id_type=MESH)

    loads = [pltpu.make_async_copy(x_ref.at[f], rows.at[f], load_sem.at[f]) for f in range(FIELDS)]
    for load in loads:
        load.start()
    clear_outside(buf, local_rows, sub, lat, size)
    none = jnp.full((sub, TILE), -1.0, jnp.float32)

    @pl.when(lat == 0)
    def _():
        edge_ref[0] = none

    @pl.when(lat == size - 1)
    def _():
        edge_ref[1] = none

    inner = (lat > 0) & (lat < size - 1)

    @pl.when(inner)
    def _():
        pl.semaphore_wait(barrier, 2)

    @pl.when(jnp.logical_not(inner))
    def _():
        pl.semaphore_wait(barrier, 1)

    copies = halo_copies(buf, local_rows, sub, lat, size, send_sem, recv_sem)
    for side, peer in ((0, lat - 1), (1, lat + 1)):
        row = 0 if side == 0 else local_rows - 1
        copies[side].append(
            pltpu.make_async_remote_copy(
                src_ref=lab_ref.at[row],
                dst_ref=edge_ref.at[1 - side],
                send_sem=lab_send.at[side],
                recv_sem=lab_recv.at[side],
                device_id=(mem, peer),
                device_id_type=MESH,
            )
        )
    for field in range(FIELDS + 1):
        if field < FIELDS:
            loads[field].wait()
            planes_from_rows(rows, buf, local_rows, sub, (field,))
        start_halo([side[field : field + 1] for side in copies], lat, size)
    finish_halo(copies, lat, size)


def second_kernel(
    size, local_rows, sub, first_ref, partner_ref, analysis_ref, lab_ref, edge_ref, buf, factor_ref,
    spread, sums, send_sem, recv_sem, sum_send, sum_recv,
):
    lat = lax.axis_index("lat")
    mem = lax.axis_index("mem")
    extent = local_rows + 2 * HALO
    barrier = pltpu.get_barrier_semaphore()
    for hop in range(1, size):
        pl.semaphore_signal(barrier, inc=1, device_id=(mem, lax.rem(lat + hop, size)), device_id_type=MESH)

    def fold(plane):
        total = plane[0:8]
        for i in range(8, sub, 8):
            total = total + plane[i : i + 8]
        return total

    energies = [jnp.zeros((8, TILE), jnp.float32) for _ in range(REGIONS)]
    counts = [jnp.zeros((8, TILE), jnp.float32) for _ in range(REGIONS)]

    def accumulate(row, carry):
        energies, counts = carry
        total = jnp.zeros((sub, TILE), jnp.float32)
        for field in range(FIELDS):
            parts = []
            for i in range(sub // 8):
                column = ((field * local_rows + row) * (sub // 8) + i) * TILE
                place = pl.ds(pl.multiple_of(column, TILE), TILE)
                parts.append(first_ref[:, place] - partner_ref[:, place])
            half = 0.5 * jnp.concatenate(parts, axis=0)
            spread[field, row] = half
            total = total + half * half
        quarter = 0.125 * total
        here = lab_ref[row]
        before = jnp.where(row == 0, edge_ref[0], lab_ref[jnp.maximum(row - 1, 0)])
        after = jnp.where(row == local_rows - 1, edge_ref[1], lab_ref[jnp.minimum(row + 1, local_rows - 1)])
        new_energies, new_counts = [], []
        for k in range(REGIONS):
            kept = jnp.where(here == k, 1.0, 0.0)
            weight = 2.0 * kept + jnp.where(before == k, 1.0, 0.0) + jnp.where(after == k, 1.0, 0.0)
            new_energies.append(energies[k] + fold(quarter * weight))
            new_counts.append(counts[k] + fold(kept))
        return new_energies, new_counts

    energies, counts = lax.fori_loop(0, local_rows, accumulate, (energies, counts))
    for k in range(REGIONS):
        sums[0, k : k + 1, :] = jnp.sum(energies[k], axis=0, keepdims=True)
        sums[0, REGIONS + k : REGIONS + k + 1, :] = jnp.sum(counts[k], axis=0, keepdims=True)

    pl.semaphore_wait(barrier, size - 1)
    sends = []
    for hop in range(1, size):
        sends.append(
            pltpu.make_async_remote_copy(
                src_ref=sums.at[0],
                dst_ref=sums.at[hop],
                send_sem=sum_send.at[hop],
                recv_sem=sum_recv.at[hop],
                device_id=(mem, lax.rem(lat + hop, size)),
                device_id_type=MESH,
            )
        )
    for copy in sends:
        copy.start()
    clear_outside(buf, local_rows, sub, lat, size)
    planes_from_rows(analysis_ref, buf, local_rows, sub)
    for copy in sends:
        copy.wait()
    total = sums[0]
    for hop in range(1, size):
        total = total + sums[hop]
    total = jnp.sum(total, axis=1, keepdims=True)
    factor = target_size / jnp.sqrt(total[:REGIONS] / total[REGIONS:] + small_eps)
    wide = jnp.broadcast_to(factor, (REGIONS, TILE))
    diagonal = lax.broadcasted_iota(jnp.int32, (REGIONS, TILE), 0) == lax.broadcasted_iota(
        jnp.int32, (REGIONS, TILE), 1
    )
    factor_ref[...] = jnp.sum(jnp.where(diagonal, wide, 0.0), axis=0, keepdims=True)[:, :REGIONS]
    lanes = [jnp.broadcast_to(wide[k : k + 1], (sub, TILE)) for k in range(REGIONS)]

    def middle(row, carry):
        here = lab_ref[row]
        scale = lanes[0]
        for k in range(1, REGIONS):
            scale = jnp.where(here == k, lanes[k], scale)
        for field in range(FIELDS):
            place = pl.ds(pl.multiple_of((field * extent + HALO + row) * sub, sub), sub)
            buf[place, :] = buf[place, :] + scale * spread[field, row]
        return carry

    lax.fori_loop(0, local_rows, middle, 0)
    copies = halo_copies(buf, local_rows, sub, lat, size, send_sem, recv_sem)
    start_halo(copies, lat, size)
    finish_halo(copies, lat, size)


def partner_fields(fields, pairing, index):
    pairs = pairs_of(lax.axis_size("mem"))
    if len(pairs) > MAX_BRANCHES:
        piece = lax.all_gather(fields, "mem", axis=0)
        return lax.dynamic_index_in_dim(piece, pairing[lax.axis_index("mem")], 0, keepdims=False)
    branches = [
        functools.partial(lax.ppermute, axis_name="mem", perm=[(a, b), (b, a)]) for a, b in pairs
    ]
    return lax.switch(index, branches, fields)


def local(replica_variables, analysis, labels, pairing):
    size = lax.axis_size("lat")
    fields, local_rows, width = analysis.shape
    sub = width // TILE
    extent = local_rows + 2 * HALO
    wide = jax.ShapeDtypeStruct((8, fields * local_rows * width // 8), jnp.float32)
    extended = jax.ShapeDtypeStruct((fields * extent * sub, TILE), jnp.float32)
    edges = jax.ShapeDtypeStruct((2, sub, TILE), jnp.float32)
    factors = jax.ShapeDtypeStruct((1, REGIONS), jnp.float32)
    label_planes = jnp.broadcast_to(labels.astype(jnp.float32)[..., None], (local_rows, sub, TILE))
    whole = pl.BlockSpec(memory_space=pltpu.VMEM)
    buffers = [
        pltpu.VMEM((fields * extent * sub, TILE), jnp.float32),
        pltpu.VMEM((extent * sub, TILE), jnp.float32),
    ]
    halo_sems = [pltpu.SemaphoreType.DMA((2, fields)), pltpu.SemaphoreType.DMA((2, fields))]
    state, edge = pl.pallas_call(
        functools.partial(first_kernel, size, local_rows, sub),
        out_shape=(extended, edges),
        in_specs=[pl.BlockSpec(memory_space=pltpu.HBM), whole],
        out_specs=(whole, whole),
        scratch_shapes=[pltpu.VMEM(analysis.shape, jnp.float32), pltpu.SemaphoreType.DMA((fields,))]
        + halo_sems
        + [pltpu.SemaphoreType.DMA((2,)), pltpu.SemaphoreType.DMA((2,))],
        compiler_params=pltpu.CompilerParams(collective_id=0, has_side_effects=True, vmem_limit_bytes=VMEM_LIMIT),
    )(replica_variables[0], label_planes)
    smem = pl.BlockSpec(memory_space=pltpu.SMEM)
    first, index = pl.pallas_call(
        functools.partial(steps_kernel, size, local_rows, sub, False),
        out_shape=(wide, jax.ShapeDtypeStruct((1, 1), jnp.int32)),
        in_specs=[whole, smem],
        out_specs=(whole, smem),
        scratch_shapes=buffers,
        compiler_params=pltpu.CompilerParams(vmem_limit_bytes=VMEM_LIMIT),
    )(state, pairing)
    partner = partner_fields(first, pairing, index[0, 0])
    state, factor = pl.pallas_call(
        functools.partial(second_kernel, size, local_rows, sub),
        out_shape=(extended, factors),
        in_specs=[whole] * 5,
        out_specs=(whole, whole),
        scratch_shapes=[
            pltpu.VMEM((fields, local_rows, sub, TILE), jnp.float32),
            pltpu.VMEM((size, 2 * REGIONS, TILE), jnp.float32),
        ]
        + halo_sems
        + [pltpu.SemaphoreType.DMA((size,)), pltpu.SemaphoreType.DMA((size,))],
        compiler_params=pltpu.CompilerParams(collective_id=1, has_side_effects=True, vmem_limit_bytes=VMEM_LIMIT),
    )(first, partner, analysis, label_planes, edge)
    closing, factor = pl.pallas_call(
        functools.partial(steps_kernel, size, local_rows, sub, True),
        out_shape=(jax.ShapeDtypeStruct(analysis.shape, jnp.float32), factors),
        in_specs=[whole] * 2,
        out_specs=(whole, whole),
        scratch_shapes=buffers,
        compiler_params=pltpu.CompilerParams(vmem_limit_bytes=VMEM_LIMIT),
    )(state, factor)
    return (closing[None], factor)


def solution(mesh):
    return jax.shard_map(
        local,
        mesh=mesh,
        in_specs=(P("mem", None, "lat", None), P(None, "lat", None), P("lat", None), P()),
        out_specs=(P("mem", None, "lat", None), P("mem", None)),
        check_vma=False,
    )
```
